32 devices in a mesh: segment: 4 (over y, x), dom: 8 (over z, core).
Axes of the slice: x: 2, y: 2, z: 4, core: 2. Of those that a mesh axis runs over, the one named last changes fastest.
Arguments:
- samples: bfloat16 [4, 4096, 512], P(None, 'dom'), may hold values from -6 to 6
- w_source: bfloat16 [4, 1, 512, 512], P('segment'), may hold values from -0.25 to 0.25
- w_self: bfloat16 [4, 1, 512, 512], P('segment'), may hold values from -0.25 to 0.25
- w_message: bfloat16 [4, 1, 512, 512], P('segment'), may hold values from -0.25 to 0.25
- w_output: bfloat16 [4, 1, 512, 512], P('segment'), may hold values from -0.25 to 0.25
- norm_gain: float32 [4, 1, 512], P('segment'), may hold values from 0.1 to 1.9
- tile_source: int32 [4, 32, 6], P('segment', 'dom'), may hold values from 0 to 31, as said below
- tile_count: int32 [4, 32], P('segment', 'dom'), may hold values from 3 to 6, as said below
- tile_value: bfloat16 [4, 32, 6, 128, 128], P('segment', 'dom'), may hold values from -0.21875 to 0.21875
Outputs:
- final: bfloat16 [4, 4096, 512], P('segment', 'dom')
The draws below stay inside these ranges and needn't reach their ends.
Inputs may be any that keep to these rules, and one draw needn't show every extreme that they name: `tile_source`: each entry for destination block b names a block among the 4 blocks that hold b's dom index (blocks (b // 4) * 4 .. + 4 - 1) or the 1 block on either side of them, counted cyclically over 32. `tile_count`: slots at or beyond the count are unused; the first block of every dom index uses all 6 slots.
All inputs are finite; a program needn't handle non-finite values.
Results may differ from the reference program's by a relative error of at most 0.013.
Values may be sent and summed in bfloat16 or wider, within the bound.
A program may use at most 64 MiB of HBM per device.

```python
import jax
import jax.numpy as jnp
from jax import lax

D = 512
BLK = 128
BD = 4
HB = 1
K = 6
LPS = 1
SAMPLES = 4
SEGMENTS = 4
NBLK = 32
NODES = 4096


def draw_tile_source(key, part):
    blocks = jnp.arange(NBLK, dtype=jnp.int32)
    base = blocks // BD * BD - HB
    offsets = jax.random.randint(jax.random.fold_in(key, 11), (SEGMENTS, NBLK, K), 0, BD + 2 * HB)
    lower = jax.random.randint(jax.random.fold_in(key, 12), (SEGMENTS, NBLK), 0, HB)
    upper = jax.random.randint(jax.random.fold_in(key, 13), (SEGMENTS, NBLK), BD + HB, BD + 2 * HB)
    own = jnp.broadcast_to(blocks % BD + HB, (SEGMENTS, NBLK))
    offsets = offsets.at[:, :, 0].set(own)
    offsets = offsets.at[:, :, 1].set(lower)
    offsets = offsets.at[:, :, 2].set(upper)
    return jnp.mod(base[None, :, None] + offsets, NBLK).astype(jnp.int32)


def draw_tile_count(key, part):
    counts = jax.random.randint(jax.random.fold_in(key, 21), (SEGMENTS, NBLK), 3, K + 1)
    first = (jnp.arange(NBLK, dtype=jnp.int32) % BD == 0)[None, :]
    return jnp.where(first, K, counts).astype(jnp.int32)


def steps_of(key, dims, shards, low, largest):
    def one(axis_at, shards_of):
        steps = jax.random.uniform(jax.random.fold_in(jax.random.fold_in(key, 6), axis_at), (shards_of,), jnp.float32, low / len(shards), largest / len(shards))
        return jnp.repeat(jnp.exp(steps), dims[axis_at] // shards_of).reshape((-1,) + (1,) * (len(dims) - axis_at - 1))

    gain = one(*shards[0])
    for cut in shards[1:]:
        gain = gain * one(*cut)
    return gain


def noise(stream_key, dims, width, limit, split=(), kind=jnp.bfloat16):
    entries = jax.random.normal(stream_key, dims, jnp.float32) * width
    if len(split) > 0:
        entries = steps_of(stream_key, dims, split, -0.22, 0.18) * entries
    return jnp.clip(entries, min=-limit, max=limit).astype(kind)


def setup_inputs(seed: int = 0) -> dict:
    arg_keys = jax.random.split(jax.random.key(seed), 10)
    samples = noise(arg_keys[0], (SAMPLES, NODES, D), 1.0, 6.0, ((1, 8),))
    w_source = noise(arg_keys[1], (SEGMENTS, LPS, D, D), D ** -0.5, 0.25, ((0, 4),))
    w_self = noise(arg_keys[2], (SEGMENTS, LPS, D, D), D ** -0.5, 0.25, ((0, 4),))
    w_message = noise(arg_keys[3], (SEGMENTS, LPS, D, D), D ** -0.5, 0.25, ((0, 4),))
    w_output = noise(arg_keys[4], (SEGMENTS, LPS, D, D), D ** -0.5, 0.25, ((0, 4),))
    norm_gain = jnp.clip(1.0 + 0.18 * jax.random.normal(arg_keys[5], (SEGMENTS, LPS, D), jnp.float32), 0.1, 1.9)
    tile_source = draw_tile_source(jax.random.fold_in(arg_keys[9], 71), 0)
    tile_count = draw_tile_count(jax.random.fold_in(arg_keys[9], 71), 0)
    tile_value = noise(arg_keys[8], (SEGMENTS, NBLK, K, BLK, BLK), (BLK * K) ** -0.5, 0.21875, ((0, 4), (1, 8)))
    return dict(samples=samples, w_source=w_source, w_self=w_self, w_message=w_message, w_output=w_output, norm_gain=norm_gain, tile_source=tile_source, tile_count=tile_count, tile_value=tile_value)


def run_layer(h, w_source, w_self, w_message, w_output, norm_gain, sources, counts, tiles):
    sender = jax.nn.silu(jnp.dot(h, w_source, preferred_element_type=jnp.float32)).astype(jnp.bfloat16)
    sender_blocks = sender.reshape(NBLK, BLK, D)
    slots = jnp.arange(K, dtype=jnp.int32)

    def one_block(packed):
        src_row, count_one, tile_set = packed
        keep = (slots < count_one).astype(jnp.float32)
        weights = tile_set.astype(jnp.float32) * keep[:, None, None]
        picked = sender_blocks[src_row.astype(jnp.int32)].astype(jnp.float32)
        return jnp.einsum('kij,kjd->id', weights, picked)
    gathered = lax.map(one_block, (sources, counts, tiles)).reshape(NODES, D).astype(jnp.bfloat16)
    mixed = jnp.dot(h, w_self, preferred_element_type=jnp.float32) + jnp.dot(gathered, w_message, preferred_element_type=jnp.float32)
    scaled = mixed / jnp.sqrt(lax.optimization_barrier(jnp.mean(mixed * mixed, axis=-1, keepdims=True)) + 1e-05) * norm_gain
    update = jax.nn.silu(scaled).astype(jnp.bfloat16)
    return (h.astype(jnp.float32) + jnp.dot(update, w_output, preferred_element_type=jnp.float32)).astype(jnp.bfloat16)

def reference(samples, w_source, w_self, w_message, w_output, norm_gain, tile_source, tile_count, tile_value):
    outputs = []
    for sample in range(SAMPLES):
        h = samples[sample]
        for section in range(SEGMENTS):
            for layer in range(LPS):
                h = run_layer(h, w_source[section, layer], w_self[section, layer], w_message[section, layer], w_output[section, layer], norm_gain[section, layer], tile_source[section], tile_count[section], tile_value[section])
        outputs.append(h)
    return jnp.stack(outputs)
```

```python
import jax
import jax.numpy as jnp
from jax import lax
from jax.sharding import PartitionSpec as P

HB = 1


def from_neighbours(cells, width):
    count = lax.axis_size("dom")
    head = cells[:width]
    tail = cells[cells.shape[0] - width :]
    before = lax.ppermute(tail, "dom", [(i, (i + 1) % count) for i in range(count)])
    after = lax.ppermute(head, "dom", [((i + 1) % count, i) for i in range(count)])
    return before, after


def dense_edges(sources, counts, tiles):
    blocks, slots, rows, _ = tiles.shape
    window = blocks + 2 * HB
    total = blocks * lax.axis_size("dom")
    first = lax.axis_index("dom") * blocks - HB
    local = jnp.mod(sources - first, total)
    used = jnp.arange(slots, dtype=jnp.int32)[None, :] < counts[:, None]
    hits = (local[:, :, None] == jnp.arange(window, dtype=jnp.int32)) & used[:, :, None]
    dense = jnp.sum(
        jnp.where(hits[:, :, None, :, None], tiles[:, :, :, None, :].astype(jnp.float32), 0.0),
        axis=1,
    )
    return dense.reshape(blocks * rows, window * rows).astype(jnp.bfloat16)


def shards(
    samples, w_source, w_self, w_message, w_output, norm_gain, tile_source, tile_count, tile_value
):
    sections = lax.axis_size("segment")
    mine = lax.axis_index("segment")
    edges = dense_edges(tile_source[0], tile_count[0], tile_value[0])
    halo = HB * tile_value.shape[-1]
    weights = jnp.concatenate([w_source[0, 0], w_self[0, 0], w_message[0, 0], w_output[0, 0]])
    weights = lax.all_gather(weights, "segment")
    edges = lax.all_gather(edges, "segment")
    gains = lax.all_gather(norm_gain[0, 0], "segment")
    h = lax.dynamic_index_in_dim(samples, mine, 0, keepdims=False)
    width = h.shape[1]
    for s in range(sections):
        wa, wb, wc, wd = (weights[s, i * width : (i + 1) * width] for i in range(4))
        sender = jax.nn.silu(jnp.dot(h, wa, preferred_element_type=jnp.float32)).astype(
            jnp.bfloat16
        )
        before, after = from_neighbours(sender, halo)
        padded = jnp.concatenate([before, sender, after])
        gathered = jnp.dot(edges[s], padded, preferred_element_type=jnp.float32).astype(
            jnp.bfloat16
        )
        mixed = jnp.dot(h, wb, preferred_element_type=jnp.float32) + jnp.dot(
            gathered, wc, preferred_element_type=jnp.float32
        )
        scale = lax.rsqrt(jnp.mean(mixed * mixed, axis=-1, keepdims=True) + 1e-05)
        update = jax.nn.silu(mixed * scale * gains[s]).astype(jnp.bfloat16)
        h = (
            h.astype(jnp.float32) + jnp.dot(update, wd, preferred_element_type=jnp.float32)
        ).astype(jnp.bfloat16)
    return h[None]


def solution(mesh):
    return jax.shard_map(
        shards,
        mesh=mesh,
        in_specs=(
            P(None, "dom", None),
            P("segment", None, None, None),
            P("segment", None, None, None),
            P("segment", None, None, None),
            P("segment", None, None, None),
            P("segment", None, None),
            P("segment", "dom", None),
            P("segment", "dom"),
            P("segment", "dom", None, None, None),
        ),
        out_specs=P("segment", "dom", None),
        check_vma=False,
    )
```

```python
import functools

import jax
import jax.numpy as jnp
from jax import lax
from jax.experimental import pallas as pl
from jax.experimental.pallas import tpu as pltpu
from jax.sharding import PartitionSpec as P

HB = 1
MATS = 4
MESH = pl.DeviceIdType.MESH
F32 = jnp.float32
BF16 = jnp.bfloat16


def silu(v):
    return v / (1.0 + jnp.exp(-v))


def mm(a, b):
    return jnp.dot(a, b, preferred_element_type=F32)


def kernel(
    doms,
    samples,
    w0,
    w1,
    w2,
    w3,
    gain,
    src,
    cnt,
    tiles,
    out,
    wbuf,
    abuf,
    sbuf,
    gbuf,
    h,
    mixed,
    load_sem,
    wsend,
    wrecv,
    zrecv,
    asend,
    arecv,
    fsend,
    gsend,
    grecv,
    hsend,
    hrecv,
):
    seg = lax.axis_index("segment")
    dom = lax.axis_index("dom")
    blocks, slots, rows, _ = tiles.shape
    n = h.shape[0]
    half = n // 2
    sx = seg + 1 - 2 * lax.rem(seg, 2)
    sy = lax.rem(seg + 2, 4)
    sz = 3 - seg
    g = lax.rem(dom, 4)
    g1 = g + 1 - 2 * lax.rem(g, 2)
    g2 = lax.rem(g + 2, 4)
    g3 = 3 - g
    sib = dom + g1 - g
    zp = dom + g2 - g
    right = lax.rem(dom + 1, doms)
    left = lax.rem(dom + doms - 1, doms)

    loads = []
    for m, w in enumerate((w0, w1, w2, w3)):
        loads.append(pltpu.make_async_copy(w.at[0, 0], wbuf.at[seg, m], load_sem.at[m]))
    loads.append(pltpu.make_async_copy(samples.at[seg], h, load_sem.at[4]))
    loads.append(pltpu.make_async_copy(gain.at[0], gbuf.at[seg], load_sem.at[5]))
    for c in loads:
        c.start()

    barrier = pltpu.get_barrier_semaphore()
    for t in (sx, sy, sz):
        pl.semaphore_signal(barrier, inc=1, device_id=(t, dom), device_id_type=MESH)
    for t in (sib, zp, left, right):
        pl.semaphore_signal(barrier, inc=1, device_id=(seg, t), device_id_type=MESH)
    for c in loads:
        c.wait()
    pl.semaphore_wait(barrier, 7)

    def remote(ref, send, recv, target):
        return pltpu.make_async_remote_copy(
            src_ref=ref,
            dst_ref=ref,
            send_sem=send,
            recv_sem=recv,
            device_id=target,
            device_id_type=MESH,
        )

    tx, ty, tz, tsib, tzp = (sx, dom), (sy, dom), (sz, dom), (seg, sib), (seg, zp)

    def rows_of(which):
        return pl.ds(which * half, half)

    def w_own(i, t):
        return remote(wbuf.at[seg, g], wsend.at[i], wrecv.at[seg, g], t)

    def a_piece(i, s, part, t):
        return remote(abuf.at[s, rows_of(part)], asend.at[i], arecv.at[s, part], t)

    def g_own(i, t):
        return remote(gbuf.at[seg], gsend.at[i], grecv.at[seg], t)

    def w_relay(s, part, t):
        return remote(wbuf.at[s, g, rows_of(part)], wsend.at[2 + part], zrecv.at[part], t)

    def forward(i, s, m, t):
        return remote(wbuf.at[s, m], fsend.at[i], wrecv.at[s, m], t)

    def w_arrived(s, m):
        remote(wbuf.at[s, m], wsend.at[0], wrecv.at[s, m], tx).wait_recv()

    def a_arrived(s, part):
        a_piece(0, s, part, tx).wait_recv()

    w_own(0, tx).start()
    w_own(1, ty).start()
    for i, t in enumerate((tx, ty, tz)):
        g_own(i, t).start()

    total = blocks * doms
    first = dom * blocks
    for b in range(blocks):
        local = [lax.rem(src[0, b, k] - first + total, total) for k in range(slots)]
        count = cnt[0, b]
        vals = [tiles[b, k].astype(F32) for k in range(slots)]
        for j in range(blocks + 2 * HB):
            want = j if j <= blocks else total - 1
            acc = jnp.zeros((rows, rows), F32)
            for k in range(slots):
                hit = jnp.logical_and(local[k] == want, k < count)
                acc = acc + vals[k] * jnp.where(hit, 1.0, 0.0)
            abuf[seg, pl.ds(b * rows, rows), pl.ds(j * rows, rows)] = acc.astype(BF16)

    a_piece(0, seg, 1, tx).start()
    a_piece(1, seg, 0, ty).start()
    a_piece(2, seg, 0, tx).start()
    a_piece(3, seg, 1, ty).start()

    def adjacent_duties():
        for i, s in enumerate((sx, sy)):
            w_arrived(s, g)
            forward(3 * i, s, g, tzp).start()
            forward(3 * i + 1, s, g, tsib).start()
        w_relay(sy, 0, tx).start()
        w_relay(sx, 1, ty).start()
        for i, s in enumerate((sx, sy)):
            w_arrived(s, g2)
            forward(3 * i + 2, s, g2, tsib).start()
        a_arrived(sy, 0)
        a_piece(4, sy, 0, tx).start()
        a_arrived(sx, 1)
        a_piece(5, sx, 1, ty).start()

    def diagonal_duties():
        for part in range(2):
            w_relay(sz, part, tx).wait_recv()
        forward(6, sz, g, tzp).start()
        forward(7, sz, g, tsib).start()
        w_arrived(sz, g2)
        forward(8, sz, g2, tsib).start()

    def halo(i, s, t, lo, to):
        return pltpu.make_async_remote_copy(
            src_ref=sbuf.at[s, pl.ds(lo, rows)],
            dst_ref=sbuf.at[s, pl.ds(to, rows)],
            send_sem=hsend.at[s, i],
            recv_sem=hrecv.at[s, i],
            device_id=t,
            device_id_type=MESH,
        )

    def halos(s):
        return (
            halo(0, s, (seg, left), 0, n),
            halo(1, s, (seg, right), n - rows, n + rows),
        )

    def section(s, carry):
        @pl.when(s == jnp.where(seg == 0, 1, 0))
        def _():
            adjacent_duties()

        @pl.when(s == sz)
        def _():
            diagonal_duties()

        @pl.when(s != seg)
        def _():
            w_arrived(s, g1)
            w_arrived(s, g3)
            remote(gbuf.at[s], gsend.at[0], grecv.at[s], tx).wait_recv()

        def send_rows(lo, size):
            v = mm(h[pl.ds(lo, size), :], wbuf[s, 0])
            sbuf[s, pl.ds(lo, size), :] = silu(v).astype(BF16)

        send_rows(0, rows)
        to_left, to_right = halos(s)
        to_left.start()
        send_rows(n - rows, rows)
        to_right.start()
        send_rows(rows, n - 2 * rows)
        mixed[...] = mm(h[...], wbuf[s, 1])

        @pl.when(jnp.logical_or(s == sx, s == sz))
        def _():
            a_arrived(s, 0)

        @pl.when(jnp.logical_or(s == sy, s == sz))
        def _():
            a_arrived(s, 1)

        near = mm(abuf[s, :, pl.ds(0, n)], sbuf[s, pl.ds(0, n), :])
        to_left.wait_recv()
        to_right.wait_recv()
        far = mm(abuf[s, :, pl.ds(n, 2 * rows)], sbuf[s, pl.ds(n, 2 * rows), :])
        gathered = (near + far).astype(BF16)
        mix = mixed[...] + mm(gathered, wbuf[s, 2])
        scale = lax.rsqrt(jnp.mean(mix * mix, axis=-1, keepdims=True) + 1e-05)
        update = silu(mix * scale * gbuf[s]).astype(BF16)
        h[...] = (h[...].astype(F32) + mm(update, wbuf[s, 3])).astype(BF16)
        return carry

    lax.fori_loop(0, 4, section, 0)
    out[...] = h[...]

    w_own(0, tx).wait_send()
    w_own(1, ty).wait_send()
    for i, t in enumerate((tx, ty, tz)):
        g_own(i, t).wait_send()
    for part in range(2):
        w_relay(sx, part, tx).wait_send()
    for i in range(6):
        a_piece(i, seg, 0, tx).wait_send()
    for i in range(9):
        forward(i, sx, g, tsib).wait_send()
    for s in range(4):
        for c in halos(s):
            c.wait_send()


def shards(
    samples, w_source, w_self, w_message, w_output, norm_gain, tile_source, tile_count, tile_value
):
    sections = lax.axis_size("segment")
    doms = lax.axis_size("dom")
    assert sections == 4 and samples.shape[0] == 4 and doms % 4 == 0
    _, n, width = samples.shape
    _, blocks, slots, rows, _ = tile_value.shape
    window = (blocks + 2 * HB) * rows
    dma = pltpu.SemaphoreType.DMA
    any_space = pl.BlockSpec(memory_space=pl.ANY)
    smem = pl.BlockSpec(memory_space=pltpu.SMEM)
    vmem = pl.BlockSpec(memory_space=pltpu.VMEM)
    out = pl.pallas_call(
        functools.partial(kernel, doms),
        out_shape=jax.ShapeDtypeStruct((n, width), BF16),
        in_specs=[any_space] * 6 + [smem, smem, vmem],
        out_specs=vmem,
        scratch_shapes=[
            pltpu.VMEM((sections, MATS, width, width), BF16),
            pltpu.VMEM((sections, n, window), BF16),
            pltpu.VMEM((sections, window, width), BF16),
            pltpu.VMEM((sections, 1, width), F32),
            pltpu.VMEM((n, width), BF16),
            pltpu.VMEM((n, width), F32),
            dma((6,)),
            dma((4,)),
            dma((sections, MATS)),
            dma((2,)),
            dma((6,)),
            dma((sections, 2)),
            dma((9,)),
            dma((3,)),
            dma((sections,)),
            dma((sections, 2)),
            dma((sections, 2)),
        ],
        compiler_params=pltpu.CompilerParams(
            collective_id=0, has_side_effects=True, vmem_limit_bytes=56 * 1024 * 1024
        ),
    )(
        samples,
        w_source,
        w_self,
        w_message,
        w_output,
        norm_gain,
        tile_source,
        tile_count,
        tile_value[0],
    )
    return out[None]


def solution(mesh):
    return jax.shard_map(
        shards,
        mesh=mesh,
        in_specs=(
            P(None, "dom", None),
            P("segment", None, None, None),
            P("segment", None, None, None),
            P("segment", None, None, None),
            P("segment", None, None, None),
            P("segment", None, None),
            P("segment", "dom", None),
            P("segment", "dom"),
            P("segment", "dom", None, None, None),
        ),
        out_specs=P("segment", "dom", None),
        check_vma=False,
    )
```

```python
import functools

import jax
import jax.numpy as jnp
from jax import lax
from jax.experimental import pallas as pl
from jax.experimental.pallas import tpu as pltpu
from jax.sharding import PartitionSpec as P

HB = 1
MATS = 4
MESH = pl.DeviceIdType.MESH
F32 = jnp.float32
BF16 = jnp.bfloat16


def silu(v):
    return v / (1.0 + jnp.exp(-v))


def mm(a, b):
    return jnp.dot(a, b, preferred_element_type=F32)


def kernel(
    doms,
    samples,
    w0,
    w1,
    w2,
    w3,
    gain,
    src,
    cnt,
    tiles,
    out,
    wbuf,
    abuf,
    sbuf,
    gbuf,
    h,
    mixed,
    load_sem,
    wsend,
    wrecv,
    zrecv,
    asend,
    arecv,
    fsend,
    gsend,
    grecv,
    hsend,
    hrecv,
):
    seg = lax.axis_index("segment")
    dom = lax.axis_index("dom")
    blocks, slots, rows, _ = tiles.shape
    n = h.shape[0]
    half = n // 2
    sx = seg + 1 - 2 * lax.rem(seg, 2)
    sy = lax.rem(seg + 2, 4)
    sz = 3 - seg
    g = lax.rem(dom, 4)
    g1 = g + 1 - 2 * lax.rem(g, 2)
    g2 = lax.rem(g + 2, 4)
    g3 = 3 - g
    sib = dom + g1 - g
    zp = dom + g2 - g
    right = lax.rem(dom + 1, doms)
    left = lax.rem(dom + doms - 1, doms)

    loads = []
    for m, w in enumerate((w0, w1, w2, w3)):
        loads.append(pltpu.make_async_copy(w.at[0, 0], wbuf.at[seg, m], load_sem.at[m]))
    loads.append(pltpu.make_async_copy(samples.at[seg], h, load_sem.at[4]))
    loads.append(pltpu.make_async_copy(gain.at[0], gbuf.at[seg], load_sem.at[5]))
    for c in loads:
        c.start()

    barrier = pltpu.get_barrier_semaphore()
    for t in (sx, sy, sz):
        pl.semaphore_signal(barrier, inc=1, device_id=(t, dom), device_id_type=MESH)
    for t in (sib, zp, left, right):
        pl.semaphore_signal(barrier, inc=1, device_id=(seg, t), device_id_type=MESH)
    for c in loads:
        c.wait()
    pl.semaphore_wait(barrier, 7)

    def remote(ref, send, recv, target):
        return pltpu.make_async_remote_copy(
            src_ref=ref,
            dst_ref=ref,
            send_sem=send,
            recv_sem=recv,
            device_id=target,
            device_id_type=MESH,
        )

    tx, ty, tz, tsib, tzp = (sx, dom), (sy, dom), (sz, dom), (seg, sib), (seg, zp)

    def rows_of(which):
        return pl.ds(which * half, half)

    def w_own(i, t):
        return remote(wbuf.at[seg, g], wsend.at[i], wrecv.at[seg, g], t)

    def a_piece(i, s, part, t):
        return remote(abuf.at[s, rows_of(part)], asend.at[i], arecv.at[s, part], t)

    def g_own(i, t):
        return remote(gbuf.at[seg], gsend.at[i], grecv.at[seg], t)

    def w_relay(s, part, t):
        return remote(wbuf.at[s, g, rows_of(part)], wsend.at[2 + part], zrecv.at[part], t)

    def forward(i, s, m, t):
        return remote(wbuf.at[s, m], fsend.at[i], wrecv.at[s, m], t)

    def w_arrived(s, m):
        remote(wbuf.at[s, m], wsend.at[0], wrecv.at[s, m], tx).wait_recv()

    def a_arrived(s, part):
        a_piece(0, s, part, tx).wait_recv()

    w_own(0, tx).start()
    w_own(1, ty).start()
    for i, t in enumerate((tx, ty, tz)):
        g_own(i, t).start()

    total = blocks * doms
    first = dom * blocks
    for b in range(blocks):
        local = [lax.rem(src[0, b, k] - first + total, total) for k in range(slots)]
        count = cnt[0, b]
        vals = [tiles[b, k].astype(F32) for k in range(slots)]
        for j in range(blocks + 2 * HB):
            want = j if j <= blocks else total - 1
            acc = jnp.zeros((rows, rows), F32)
            for k in range(slots):
                hit = jnp.logical_and(local[k] == want, k < count)
                acc = acc + vals[k] * jnp.where(hit, 1.0, 0.0)
            abuf[seg, pl.ds(b * rows, rows), pl.ds(j * rows, rows)] = acc.astype(BF16)

    hold_x = sy < seg
    hold_y = sx < seg

    def own_x(first, second):
        if first:
            a_piece(0, seg, 1, tx).start()
        if second:
            a_piece(2, seg, 0, tx).start()

    def own_y(first, second):
        if first:
            a_piece(1, seg, 0, ty).start()
        if second:
            a_piece(3, seg, 1, ty).start()

    @pl.when(seg == 0)
    def _():
        own_x(True, False)
        own_y(True, False)

    lowest = jnp.where(seg == 0, 1, 0)

    def weight_duties():
        w_arrived(sx, g)
        w_arrived(sy, g)
        w_relay(sy, 0, tx).start()
        w_relay(sx, 1, ty).start()

        @pl.when(seg == 0)
        def _():
            own_x(False, True)
            own_y(False, True)

        @pl.when(jnp.logical_and(seg != 0, jnp.logical_not(hold_x)))
        def _():
            own_x(True, True)

        @pl.when(jnp.logical_and(seg != 0, jnp.logical_not(hold_y)))
        def _():
            own_y(True, True)

        for k in range(3):
            s = k + jnp.where(seg <= k, 1, 0)

            @pl.when(s == sz)
            def _():
                for part in range(2):
                    w_relay(sz, part, tx).wait_recv()

            forward(3 * k, s, g, tzp).start()
            forward(3 * k + 1, s, g, tsib).start()
        w_arrived(lowest, g2)
        forward(2, lowest, g2, tsib).start()

    def relay_from_y():
        a_arrived(sy, 0)
        a_piece(4, sy, 0, tx).start()

        @pl.when(hold_x)
        def _():
            own_x(True, True)

    def relay_from_x():
        a_arrived(sx, 1)
        a_piece(5, sx, 1, ty).start()

        @pl.when(hold_y)
        def _():
            own_y(True, True)

    ends = jnp.logical_or(seg == 0, seg == 3)
    from_x_at = jnp.where(ends, 1, jnp.where(seg == 1, 0, 2))
    from_y_at = jnp.where(ends, 1, jnp.where(seg == 1, 2, 0))

    def halo(i, s, t, lo, to):
        return pltpu.make_async_remote_copy(
            src_ref=sbuf.at[s, pl.ds(lo, rows)],
            dst_ref=sbuf.at[s, pl.ds(to, rows)],
            send_sem=hsend.at[s, i],
            recv_sem=hrecv.at[s, i],
            device_id=t,
            device_id_type=MESH,
        )

    def halos(s):
        return (
            halo(0, s, (seg, left), 0, n),
            halo(1, s, (seg, right), n - rows, n + rows),
        )

    def section(s, carry):
        @pl.when(s == lowest)
        def _():
            weight_duties()

        @pl.when(s == from_y_at)
        def _():
            relay_from_y()

        @pl.when(s == from_x_at)
        def _():
            relay_from_x()

        @pl.when(s != seg)
        def _():
            w_arrived(s, g1)
            w_arrived(s, g3)
            remote(gbuf.at[s], gsend.at[0], grecv.at[s], tx).wait_recv()

        def send_rows(lo, size):
            v = mm(h[pl.ds(lo, size), :], wbuf[s, 0])
            sbuf[s, pl.ds(lo, size), :] = silu(v).astype(BF16)

        send_rows(0, rows)
        to_left, to_right = halos(s)
        to_left.start()
        send_rows(n - rows, rows)
        to_right.start()
        send_rows(rows, n - 2 * rows)
        mixed[...] = mm(h[...], wbuf[s, 1])

        @pl.when(jnp.logical_or(s == sx, s == sz))
        def _():
            a_arrived(s, 0)

        @pl.when(jnp.logical_or(s == sy, s == sz))
        def _():
            a_arrived(s, 1)

        near = mm(abuf[s, :, pl.ds(0, n)], sbuf[s, pl.ds(0, n), :])

        later = s + 1

        @pl.when(jnp.logical_and(later < 4, jnp.logical_and(later != seg, later != lowest)))
        def _():
            w_arrived(later, g2)
            forward(jnp.where(later - jnp.where(later > seg, 1, 0) == 1, 5, 8), later, g2, tsib).start()

        to_left.wait_recv()
        to_right.wait_recv()
        far = mm(abuf[s, :, pl.ds(n, 2 * rows)], sbuf[s, pl.ds(n, 2 * rows), :])
        gathered = (near + far).astype(BF16)
        mix = mixed[...] + mm(gathered, wbuf[s, 2])
        scale = lax.rsqrt(jnp.mean(mix * mix, axis=-1, keepdims=True) + 1e-05)
        update = silu(mix * scale * gbuf[s]).astype(BF16)
        h[...] = (h[...].astype(F32) + mm(update, wbuf[s, 3])).astype(BF16)
        return carry

    lax.fori_loop(0, 4, section, 0)
    out[...] = h[...]

    w_own(0, tx).wait_send()
    w_own(1, ty).wait_send()
    for i, t in enumerate((tx, ty, tz)):
        g_own(i, t).wait_send()
    for part in range(2):
        w_relay(sx, part, tx).wait_send()
    for i in range(6):
        a_piece(i, seg, 0, tx).wait_send()
    for i in range(9):
        forward(i, sx, g, tsib).wait_send()
    for s in range(4):
        for c in halos(s):
            c.wait_send()


def shards(
    samples, w_source, w_self, w_message, w_output, norm_gain, tile_source, tile_count, tile_value
):
    sections = lax.axis_size("segment")
    doms = lax.axis_size("dom")
    assert sections == 4 and samples.shape[0] == 4 and doms % 4 == 0
    _, n, width = samples.shape
    _, blocks, slots, rows, _ = tile_value.shape
    window = (blocks + 2 * HB) * rows
    dma = pltpu.SemaphoreType.DMA
    any_space = pl.BlockSpec(memory_space=pl.ANY)
    smem = pl.BlockSpec(memory_space=pltpu.SMEM)
    vmem = pl.BlockSpec(memory_space=pltpu.VMEM)
    out = pl.pallas_call(
        functools.partial(kernel, doms),
        out_shape=jax.ShapeDtypeStruct((n, width), BF16),
        in_specs=[any_space] * 6 + [smem, smem, vmem],
        out_specs=vmem,
        scratch_shapes=[
            pltpu.VMEM((sections, MATS, width, width), BF16),
            pltpu.VMEM((sections, n, window), BF16),
            pltpu.VMEM((sections, window, width), BF16),
            pltpu.VMEM((sections, 1, width), F32),
            pltpu.VMEM((n, width), BF16),
            pltpu.VMEM((n, width), F32),
            dma((6,)),
            dma((4,)),
            dma((sections, MATS)),
            dma((2,)),
            dma((6,)),
            dma((sections, 2)),
            dma((9,)),
            dma((3,)),
            dma((sections,)),
            dma((sections, 2)),
            dma((sections, 2)),
        ],
        compiler_params=pltpu.CompilerParams(
            collective_id=0, has_side_effects=True, vmem_limit_bytes=56 * 1024 * 1024
        ),
    )(
        samples,
        w_source,
        w_self,
        w_message,
        w_output,
        norm_gain,
        tile_source,
        tile_count,
        tile_value[0],
    )
    return out[None]


def solution(mesh):
    return jax.shard_map(
        shards,
        mesh=mesh,
        in_specs=(
            P(None, "dom", None),
            P("segment", None, None, None),
            P("segment", None, None, None),
            P("segment", None, None, None),
            P("segment", None, None, None),
            P("segment", None, None),
            P("segment", "dom", None),
            P("segment", "dom"),
            P("segment", "dom", None, None, None),
        ),
        out_specs=P("segment", "dom", None),
        check_vma=False,
    )
```

```python
import functools

import jax
import jax.numpy as jnp
from jax import lax
from jax.experimental import pallas as pl
from jax.experimental.pallas import tpu as pltpu
from jax.sharding import PartitionSpec as P

HB = 1
MATS = 4
MESH = pl.DeviceIdType.MESH
F32 = jnp.float32
BF16 = jnp.bfloat16


def silu(v):
    return v / (1.0 + jnp.exp(-v))


def mm(a, b):
    return jnp.dot(a, b, preferred_element_type=F32)


def kernel(
    doms,
    samples,
    w0,
    w1,
    w2,
    w3,
    gain,
    src,
    cnt,
    tiles,
    out,
    wbuf,
    abuf,
    sbuf,
    gbuf,
    h,
    mixed,
    load_sem,
    wsend,
    wrecv,
    zrecv,
    asend,
    arecv,
    fsend,
    gsend,
    grecv,
    hsend,
    hrecv,
):
    seg = lax.axis_index("segment")
    dom = lax.axis_index("dom")
    blocks, slots, rows, _ = tiles.shape
    n = h.shape[0]
    half = n // 2
    sx = seg + 1 - 2 * lax.rem(seg, 2)
    sy = lax.rem(seg + 2, 4)
    sz = 3 - seg
    g = lax.rem(dom, 4)
    g1 = g + 1 - 2 * lax.rem(g, 2)
    g2 = lax.rem(g + 2, 4)
    g3 = 3 - g
    sib = dom + g1 - g
    zp = dom + g2 - g
    right = lax.rem(dom + 1, doms)
    left = lax.rem(dom + doms - 1, doms)

    loads = []
    for m, w in enumerate((w0, w1, w2, w3)):
        loads.append(pltpu.make_async_copy(w.at[0, 0], wbuf.at[seg, m], load_sem.at[m]))
    loads.append(pltpu.make_async_copy(samples.at[seg], h, load_sem.at[4]))
    loads.append(pltpu.make_async_copy(gain.at[0], gbuf.at[seg], load_sem.at[5]))
    for c in loads:
        c.start()

    barrier = pltpu.get_barrier_semaphore()
    for t in (sx, sy, sz):
        pl.semaphore_signal(barrier, inc=1, device_id=(t, dom), device_id_type=MESH)
    for t in (sib, zp, left, right):
        pl.semaphore_signal(barrier, inc=1, device_id=(seg, t), device_id_type=MESH)
    for c in loads:
        c.wait()
    pl.semaphore_wait(barrier, 7)

    def remote(ref, send, recv, target):
        return pltpu.make_async_remote_copy(
            src_ref=ref,
            dst_ref=ref,
            send_sem=send,
            recv_sem=recv,
            device_id=target,
            device_id_type=MESH,
        )

    tx, ty, tz, tsib, tzp = (sx, dom), (sy, dom), (sz, dom), (seg, sib), (seg, zp)

    def rows_of(which):
        return pl.ds(which * half, half)

    def w_own(i, t):
        return remote(wbuf.at[seg, g], wsend.at[i], wrecv.at[seg, g], t)

    def a_piece(i, s, part, t):
        return remote(abuf.at[s, rows_of(part)], asend.at[i], arecv.at[s, part], t)

    def g_own(i, t):
        return remote(gbuf.at[seg], gsend.at[i], grecv.at[seg], t)

    def w_relay(s, part, t):
        return remote(wbuf.at[s, g, rows_of(part)], wsend.at[2 + part], zrecv.at[part], t)

    def forward(i, s, m, t):
        return remote(wbuf.at[s, m], fsend.at[i], wrecv.at[s, m], t)

    def w_arrived(s, m):
        remote(wbuf.at[s, m], wsend.at[0], wrecv.at[s, m], tx).wait_recv()

    def a_arrived(s, part):
        a_piece(0, s, part, tx).wait_recv()

    w_own(0, tx).start()
    w_own(1, ty).start()
    for i, t in enumerate((tx, ty, tz)):
        g_own(i, t).start()

    total = blocks * doms
    first = dom * blocks
    for b in range(blocks):
        local = [lax.rem(src[0, b, k] - first + total, total) for k in range(slots)]
        count = cnt[0, b]
        vals = [tiles[b, k].astype(F32) for k in range(slots)]
        for j in range(blocks + 2 * HB):
            want = j if j <= blocks else total - 1
            acc = jnp.zeros((rows, rows), F32)
            for k in range(slots):
                hit = jnp.logical_and(local[k] == want, k < count)
                acc = acc + vals[k] * jnp.where(hit, 1.0, 0.0)
            abuf[seg, pl.ds(b * rows, rows), pl.ds(j * rows, rows)] = acc.astype(BF16)

    a_piece(0, seg, 1, tx).start()
    a_piece(1, seg, 0, ty).start()
    a_piece(2, seg, 0, tx).start()
    a_piece(3, seg, 1, ty).start()

    def adjacent_duties():
        for i, s in enumerate((sx, sy)):
            w_arrived(s, g)
            forward(3 * i, s, g, tzp).start()
            forward(3 * i + 1, s, g, tsib).start()
        w_relay(sy, 0, tx).start()
        w_relay(sx, 1, ty).start()
        for i, s in enumerate((sx, sy)):
            w_arrived(s, g2)
            forward(3 * i + 2, s, g2, tsib).start()
        a_arrived(sy, 0)
        a_piece(4, sy, 0, tx).start()
        a_arrived(sx, 1)
        a_piece(5, sx, 1, ty).start()

    def diagonal_duties():
        for part in range(2):
            w_relay(sz, part, tx).wait_recv()
        forward(6, sz, g, tzp).start()
        forward(7, sz, g, tsib).start()

    def diagonal_last():
        w_arrived(sz, g2)
        forward(8, sz, g2, tsib).start()

    def halo(i, s, t, lo, to):
        return pltpu.make_async_remote_copy(
            src_ref=sbuf.at[s, pl.ds(lo, rows)],
            dst_ref=sbuf.at[s, pl.ds(to, rows)],
            send_sem=hsend.at[s, i],
            recv_sem=hrecv.at[s, i],
            device_id=t,
            device_id_type=MESH,
        )

    def halos(s):
        return (
            halo(0, s, (seg, left), 0, n),
            halo(1, s, (seg, right), n - rows, n + rows),
        )

    def section(s, carry):
        @pl.when(s == jnp.where(seg == 0, 1, 0))
        def _():
            adjacent_duties()
            diagonal_duties()

        @pl.when(s == sz)
        def _():
            diagonal_last()

        @pl.when(s != seg)
        def _():
            w_arrived(s, g1)
            w_arrived(s, g3)
            remote(gbuf.at[s], gsend.at[0], grecv.at[s], tx).wait_recv()

        def send_rows(lo, size):
            v = mm(h[pl.ds(lo, size), :], wbuf[s, 0])
            sbuf[s, pl.ds(lo, size), :] = silu(v).astype(BF16)

        send_rows(0, rows)
        to_left, to_right = halos(s)
        to_left.start()
        send_rows(n - rows, rows)
        to_right.start()
        send_rows(rows, n - 2 * rows)
        mixed[...] = mm(h[...], wbuf[s, 1])

        @pl.when(jnp.logical_or(s == sx, s == sz))
        def _():
            a_arrived(s, 0)

        @pl.when(jnp.logical_or(s == sy, s == sz))
        def _():
            a_arrived(s, 1)

        near = mm(abuf[s, :, pl.ds(0, n)], sbuf[s, pl.ds(0, n), :])
        to_left.wait_recv()
        to_right.wait_recv()
        far = mm(abuf[s, :, pl.ds(n, 2 * rows)], sbuf[s, pl.ds(n, 2 * rows), :])
        gathered = (near + far).astype(BF16)
        mix = mixed[...] + mm(gathered, wbuf[s, 2])
        scale = lax.rsqrt(jnp.mean(mix * mix, axis=-1, keepdims=True) + 1e-05)
        update = silu(mix * scale * gbuf[s]).astype(BF16)
        h[...] = (h[...].astype(F32) + mm(update, wbuf[s, 3])).astype(BF16)
        return carry

    lax.fori_loop(0, 4, section, 0)
    final = pltpu.make_async_copy(h, out.at[0], load_sem.at[0])
    final.start()

    w_own(0, tx).wait_send()
    w_own(1, ty).wait_send()
    for i, t in enumerate((tx, ty, tz)):
        g_own(i, t).wait_send()
    for part in range(2):
        w_relay(sx, part, tx).wait_send()
    for i in range(6):
        a_piece(i, seg, 0, tx).wait_send()
    for i in range(9):
        forward(i, sx, g, tsib).wait_send()
    for s in range(4):
        for c in halos(s):
            c.wait_send()
    final.wait()


def shards(
    samples, w_source, w_self, w_message, w_output, norm_gain, tile_source, tile_count, tile_value
):
    sections = lax.axis_size("segment")
    doms = lax.axis_size("dom")
    assert sections == 4 and samples.shape[0] == 4 and doms % 4 == 0
    _, n, width = samples.shape
    _, blocks, slots, rows, _ = tile_value.shape
    window = (blocks + 2 * HB) * rows
    dma = pltpu.SemaphoreType.DMA
    any_space = pl.BlockSpec(memory_space=pl.ANY)
    smem = pl.BlockSpec(memory_space=pltpu.SMEM)
    vmem = pl.BlockSpec(memory_space=pltpu.VMEM)
    out = pl.pallas_call(
        functools.partial(kernel, doms),
        out_shape=jax.ShapeDtypeStruct((1, n, width), BF16),
        in_specs=[any_space] * 6 + [smem, smem, vmem],
        out_specs=any_space,
        scratch_shapes=[
            pltpu.VMEM((sections, MATS, width, width), BF16),
            pltpu.VMEM((sections, n, window), BF16),
            pltpu.VMEM((sections, window, width), BF16),
            pltpu.VMEM((sections, 1, width), F32),
            pltpu.VMEM((n, width), BF16),
            pltpu.VMEM((n, width), F32),
            dma((6,)),
            dma((4,)),
            dma((sections, MATS)),
            dma((2,)),
            dma((6,)),
            dma((sections, 2)),
            dma((9,)),
            dma((3,)),
            dma((sections,)),
            dma((sections, 2)),
            dma((sections, 2)),
        ],
        compiler_params=pltpu.CompilerParams(
            collective_id=0, has_side_effects=True, vmem_limit_bytes=56 * 1024 * 1024
        ),
    )(
        samples,
        w_source,
        w_self,
        w_message,
        w_output,
        norm_gain,
        tile_source,
        tile_count,
        tile_value[0],
    )
    return out


def solution(mesh):
    return jax.shard_map(
        shards,
        mesh=mesh,
        in_specs=(
            P(None, "dom", None),
            P("segment", None, None, None),
            P("segment", None, None, None),
            P("segment", None, None, None),
            P("segment", None, None, None),
            P("segment", None, None),
            P("segment", "dom", None),
            P("segment", "dom"),
            P("segment", "dom", None, None, None),
        ),
        out_specs=P("segment", "dom", None),
        check_vma=False,
    )
```
